32 devices in a mesh: tier: 8 (over z, y), mat: 4 (over x, core).
Axes of the slice: x: 2, y: 2, z: 4, core: 2. Of those that a mesh axis runs over, the one named last changes fastest.
Arguments:
- costate: bfloat16 [128, 2, 256, 256], P(('tier', 'mat')), may hold values from -6 to 6
- hamiltonian: bfloat16 [256, 256], replicated, may hold values from -0.375 to 0.375
- couplers: bfloat16 [3, 256, 256], replicated, may hold values from -0.375 to 0.375
- damping: float32 [12], replicated, may hold values from 0.05 to 0.5
- coupling: float32 [2, 12], replicated, may hold values from -0.9 to 0.9
- levels: int32 [128, 12], P(('tier', 'mat')), may hold values from 0 to 3
- neighbour_slot: int32 [128, 24], P(('tier', 'mat')), may hold values from 0 to 15
- neighbour_mode: int32 [128, 24], P(('tier', 'mat')), may hold values from 0 to 11
- neighbour_flag: int32 [128, 24], P(('tier', 'mat')), may hold values from -1 to 1
- send_index: int32 [32, 16], P(('tier', 'mat')), may hold values from 0 to 3
Outputs:
- increment: float32 [128, 2, 256, 256], P(('tier', 'mat'))
- bath_gradient: float32 [12], replicated
The draws below stay inside these ranges and needn't reach their ends.
All inputs are finite; a program needn't handle non-finite values.
Results may differ from the reference program's by a relative error of at most 0.0053.
Values may be sent and summed in bfloat16 or wider, within the bound.
A program may use at most 128 MiB of HBM per device.

```python
import math
import jax
import jax.numpy as jnp
from jax import lax

NL = 256
MODES = 12
OPS = 3
NEIGH = 24
CAP = 2
MB_DEV = 4
BLOCKS = 32
ADOS = 128
SLOTS = 16
N_MAT = 4


def set_ends(array, key, low, high):
    extent = array.shape
    spot = [jax.random.randint(jax.random.fold_in(key, axis), (), 0, extent[axis]) for axis in range(len(extent))]
    array = array.at[tuple(spot)].set(low)
    longest = extent.index(max(extent))
    spot[longest] = (spot[longest] + 1) % extent[longest]
    return array.at[tuple(spot)].set(high)


def steps_of(stream_key, extent, shards, low, largest):
    level = 1.0
    for dim, blocks in shards:
        heights = jax.random.uniform(jax.random.fold_in(jax.random.fold_in(stream_key, 6), dim), (blocks,), jnp.float32, low / len(shards), largest / len(shards))
        level = level * jnp.repeat(jnp.exp(heights), extent[dim] // blocks).reshape((-1,) + (1,) * (len(extent) - 1 - dim))
    return level


def noise(own_key, dims, spread, limit, cuts=(), kind=jnp.bfloat16):
    factor_of = steps_of(own_key, dims, cuts, -0.22, 0.18) if cuts else 1.0
    entries = jax.random.normal(own_key, dims, jnp.float32) * spread * factor_of
    return jnp.minimum(jnp.maximum(entries, -limit), limit).astype(kind)


def setup_inputs(seed: int = 0) -> dict:
    seeds = jax.random.split(jax.random.key(seed), 11)
    return {
        "costate": noise(seeds[0], (ADOS, 2, NL, NL), 1.0, 6.0, ((0, 32),)),
        "hamiltonian": noise(seeds[1], (NL, NL), NL ** -0.5, 0.375),
        "couplers": noise(seeds[2], (OPS, NL, NL), NL ** -0.5, 0.375),
        "damping": jnp.clip(jnp.exp(jax.random.uniform(seeds[3], (MODES,), jnp.float32, math.log(0.05), math.log(0.5))), 0.05, 0.5),
        "coupling": noise(seeds[4], (2, MODES), 0.3, 0.9, (), jnp.float32),
        "levels": set_ends(jax.random.randint(seeds[5], (ADOS, MODES), 0, 4), jax.random.fold_in(seeds[5], 1), 0, 3).astype(jnp.int32),
        "neighbour_slot": set_ends(jax.random.randint(seeds[6], (ADOS, NEIGH), 0, SLOTS), jax.random.fold_in(seeds[6], 1), 0, SLOTS - 1).astype(jnp.int32),
        "neighbour_mode": set_ends(jax.random.randint(seeds[7], (ADOS, NEIGH), 0, MODES), jax.random.fold_in(seeds[7], 1), 0, MODES - 1).astype(jnp.int32),
        "neighbour_flag": set_ends(jax.random.randint(seeds[8], (ADOS, NEIGH), -1, 2), jax.random.fold_in(seeds[8], 1), -1, 1).astype(jnp.int32),
        "send_index": set_ends(jax.random.randint(seeds[9], (BLOCKS, SLOTS), 0, MB_DEV), jax.random.fold_in(seeds[9], 1), 0, MB_DEV - 1).astype(jnp.int32),
    }


def symmetric(weight):
    square = weight.astype(jnp.float32)
    return ((square + jnp.swapaxes(square, -1, -2)) * 0.5).astype(jnp.bfloat16)

def evaluate(state, operators, damping, coupling, levels, neighbour_slot, neighbour_mode, neighbour_flag, send_index):
    high = lax.Precision.HIGHEST
    opfloat = operators.astype(jnp.float32)

    def single(index):
        block = index // MB_DEV
        tier_here = block // N_MAT
        group = block % N_MAT
        slot = neighbour_slot[index]
        provider = slot // CAP * N_MAT + group
        position = slot % CAP
        source = (provider * MB_DEV + send_index[provider, tier_here * CAP + position]).astype(jnp.int32)
        gathered = state[source].astype(jnp.float32)
        own = state[index].astype(jnp.float32)
        mode = neighbour_mode[index]
        flag = neighbour_flag[index]
        live = (flag >= 0).astype(jnp.float32)
        weight = jnp.sqrt(1.0 + levels[index][mode].astype(jnp.float32)) * live
        coup_real = coupling[0][mode] * weight
        coup_imag = coupling[1][mode] * weight
        right_imag = jnp.where(flag == 1, coup_imag, -coup_imag)
        select = (mode[None, :] % 3 == jnp.arange(3)[:, None]).astype(jnp.float32)

        def combine(real_part, imag_part):
            creal = select * real_part[None, :]
            cimag = select * imag_part[None, :]
            sreal = jnp.einsum('qe,eij->qij', creal, gathered[:, 0], precision=high) - jnp.einsum('qe,eij->qij', cimag, gathered[:, 1], precision=high)
            simag = jnp.einsum('qe,eij->qij', creal, gathered[:, 1], precision=high) + jnp.einsum('qe,eij->qij', cimag, gathered[:, 0], precision=high)
            return jnp.stack([sreal, simag], 1).astype(jnp.bfloat16)
        left_in = combine(coup_real, coup_imag)
        right_in = combine(coup_real, right_imag)
        rotated = jnp.stack([-state[index][1], state[index][0]])[None]
        left_all = jnp.concatenate([rotated, left_in], 0).astype(jnp.float32)
        right_all = jnp.concatenate([rotated, right_in], 0).astype(jnp.float32)
        left = jnp.einsum('oij,opjk->pik', opfloat, left_all, precision=high)
        right = jnp.einsum('opij,ojk->pik', right_all, opfloat, precision=high)
        decay = jnp.sum(levels[index].astype(jnp.float32) * damping)
        rate = left - right - decay * own
        correlation = jnp.einsum('pij,epij->e', own, gathered, precision=high)
        onehot = (mode[:, None] == jnp.arange(MODES)[None, :]).astype(jnp.float32)
        grad = jnp.dot(correlation * weight / NL, onehot, precision=high)
        return (rate, grad)
    rates, grads = lax.map(single, jnp.arange(state.shape[0], dtype=jnp.int32))
    return (rates, lax.optimization_barrier(jnp.sum(grads, 0)))

def reference(costate, hamiltonian, couplers, damping, coupling, levels, neighbour_slot, neighbour_mode, neighbour_flag, send_index):
    operators = jnp.concatenate([symmetric(hamiltonian)[None], symmetric(couplers)], 0)
    first, grad_first = evaluate(costate, operators, damping, coupling, levels, neighbour_slot, neighbour_mode, neighbour_flag, send_index)
    middle = (costate.astype(jnp.float32) + 0.125 * first).astype(jnp.bfloat16)
    second, grad_second = evaluate(middle, operators, damping, coupling, levels, neighbour_slot, neighbour_mode, neighbour_flag, send_index)
    return (0.25 * second, grad_first + grad_second)
```

```python
import functools

import jax
import jax.numpy as jnp
from jax import lax
from jax.experimental import pallas as pl
from jax.experimental.pallas import tpu as pltpu
from jax.sharding import PartitionSpec as P

ROWS = 16
F32 = jnp.float32
BF16 = jnp.bfloat16


def symmetric(weight):
    square = weight.astype(F32)
    return ((square + jnp.swapaxes(square, -1, -2)) * 0.5).astype(BF16)


def coefficients(coupling, levels, slot, mode, flag, slots):
    modes = levels.shape[1]
    mode_hot = mode[:, :, None] == jnp.arange(modes)[None, None, :]

    def pick(values):
        return jnp.sum(jnp.where(mode_hot, values, 0.0), -1)

    live = (flag >= 0).astype(F32)
    weight = jnp.sqrt(1.0 + pick(levels.astype(F32)[:, None, :])) * live
    real = pick(coupling[0][None, None, :]) * weight
    imag = pick(coupling[1][None, None, :]) * weight
    other = jnp.where(flag == 1, imag, -imag)
    op_hot = mode[:, :, None] % 3 == jnp.arange(3)[None, None, :]
    slot_hot = slot[:, :, None] == jnp.arange(slots)[None, None, :]
    both = op_hot[:, :, :, None] & slot_hot[:, :, None, :]

    def spread(values):
        return jnp.sum(jnp.where(both, values[:, :, None, None], 0.0), 1)

    creal, left, right = spread(real), spread(imag), spread(other)

    def parts(cimag):
        return jnp.stack([jnp.stack([creal, -cimag], -1), jnp.stack([cimag, creal], -1)], 1)

    table = jnp.stack([parts(left), parts(right)], 1)
    table = table.reshape(-1, slots * 2).astype(BF16)
    pair = mode_hot[:, :, :, None] & slot_hot[:, :, None, :]
    corr = jnp.sum(jnp.where(pair, weight[:, :, None, None], 0.0), 1)
    return table, corr


def blown_up(table):
    tall, wide = table.shape
    down = (jnp.arange(tall * ROWS)[:, None] // ROWS == jnp.arange(tall)[None, :]).astype(BF16)
    along = (jnp.arange(wide)[:, None] == jnp.arange(wide * ROWS)[None, :] // ROWS).astype(BF16)
    big = jnp.dot(down, table, preferred_element_type=F32).astype(BF16)
    big = jnp.dot(big, along, preferred_element_type=F32)
    keep = jnp.arange(tall * ROWS)[:, None] % ROWS == jnp.arange(wide * ROWS)[None, :] % ROWS
    return jnp.where(keep, big, 0.0).astype(BF16)


def section_kernel(first, decay_ref, coef_ref, state_ref, recv_ref, ops_ref, before_ref, out_ref, corr_ref, mixed):
    count, _, width, _ = state_ref.shape
    slots = recv_ref.shape[0]
    corr_ref[...] = before_ref[...]

    @pl.loop(0, width // ROWS)
    def _(step):
        rows = pl.ds(pl.multiple_of(step * ROWS, ROWS), ROWS)
        chunk = recv_ref[:, :, rows, :]
        sums = jnp.dot(
            coef_ref[...], chunk.reshape(slots * 2 * ROWS, width), preferred_element_type=F32
        ).astype(BF16)
        mixed[:, :, :, :, rows, :] = sums.reshape(count, 2, 2, 3, ROWS, width)
        for part in range(2):
            corr_ref[...] += lax.dot_general(
                state_ref[:, part, rows, :].reshape(count * ROWS, width),
                chunk[:, part].reshape(slots * ROWS, width),
                (((1,), (1,)), ((), ())),
                preferred_element_type=F32,
            )

    @pl.loop(0, count)
    def _(n):
        decay = decay_ref[n]
        for part in range(2):
            turned = -state_ref[n, 1] if part == 0 else state_ref[n, 0]
            rate = jnp.dot(ops_ref[0], turned, preferred_element_type=F32)
            for q in range(3):
                rate += jnp.dot(ops_ref[1 + q], mixed[n, 0, part, q], preferred_element_type=F32)
            back = jnp.dot(turned, ops_ref[0], preferred_element_type=F32)
            for q in range(3):
                back += jnp.dot(mixed[n, 1, part, q], ops_ref[1 + q], preferred_element_type=F32)
            own = state_ref[n, part].astype(F32)
            rate = rate - back - decay * own
            if first:
                out_ref[n, part] = (own + 0.125 * rate).astype(BF16)
            else:
                out_ref[n, part] = 0.25 * rate


def section(first, decay, coef, state, received, operators, before):
    count, _, width, _ = state.shape
    vmem = pl.BlockSpec(memory_space=pltpu.VMEM)
    return pl.pallas_call(
        functools.partial(section_kernel, first),
        out_shape=(
            jax.ShapeDtypeStruct(state.shape, BF16 if first else F32),
            jax.ShapeDtypeStruct(before.shape, F32),
        ),
        in_specs=[pl.BlockSpec(memory_space=pltpu.SMEM)] + [vmem] * 5,
        out_specs=(vmem, vmem),
        scratch_shapes=[pltpu.VMEM((count, 2, 2, 3, width, width), BF16)],
        compiler_params=pltpu.CompilerParams(vmem_limit_bytes=48 << 20),
        name="section_first" if first else "section_second",
    )(decay, coef, state, received, operators, before)


def receive(outgoing):
    return lax.all_to_all(outgoing, "tier", split_axis=0, concat_axis=0, tiled=True)


def per_device(
    costate,
    hamiltonian,
    couplers,
    damping,
    coupling,
    levels,
    neighbour_slot,
    neighbour_mode,
    neighbour_flag,
    send_index,
):
    count, _, width, _ = costate.shape
    slots = send_index.shape[1]
    received = receive(costate[send_index[0]])
    operators = jnp.concatenate([symmetric(hamiltonian)[None], symmetric(couplers)], 0)
    table, corr_weight = coefficients(
        coupling, levels, neighbour_slot, neighbour_mode, neighbour_flag, slots
    )
    coef = blown_up(table)
    decay = jnp.sum(levels.astype(F32) * damping[None, :], 1)
    corr = jnp.zeros((count * ROWS, slots * ROWS), F32)
    middle, corr = section(True, decay, coef, costate, received, operators, corr)
    received = receive(middle[send_index[0]])
    increment, corr = section(False, decay, coef, middle, received, operators, corr)
    row = jnp.arange(count * ROWS)[:, None]
    column = jnp.arange(slots * ROWS)[None, :]
    corr = jnp.where(row % ROWS == column % ROWS, corr, 0.0)
    pairs = jnp.sum(corr.reshape(count, ROWS, slots, ROWS), (1, 3)) / width
    grads = jnp.sum(pairs[:, None, :] * corr_weight, (0, 2))
    return increment, lax.psum(grads, ("tier", "mat"))


def solution(mesh):
    blocks = P(("tier", "mat"), None)
    return jax.shard_map(
        per_device,
        mesh=mesh,
        in_specs=(P(("tier", "mat"), None, None, None), P(), P(), P(), P()) + (blocks,) * 5,
        out_specs=(P(("tier", "mat"), None, None, None), P()),
        check_vma=False,
    )
```

```python
import functools

import jax
import jax.numpy as jnp
from jax import lax
from jax.experimental import pallas as pl
from jax.experimental.pallas import tpu as pltpu
from jax.sharding import PartitionSpec as P

ROWS = 16
F32 = jnp.float32
BF16 = jnp.bfloat16
MESH = pl.DeviceIdType.MESH


def symmetric(weight):
    square = weight.astype(F32)
    return ((square + jnp.swapaxes(square, -1, -2)) * 0.5).astype(BF16)


def coefficients(coupling, levels, slot, mode, flag, slots):
    modes = levels.shape[1]
    mode_hot = mode[:, :, None] == jnp.arange(modes)[None, None, :]

    def pick(values):
        return jnp.sum(jnp.where(mode_hot, values, 0.0), -1)

    live = (flag >= 0).astype(F32)
    weight = jnp.sqrt(1.0 + pick(levels.astype(F32)[:, None, :])) * live
    real = pick(coupling[0][None, None, :]) * weight
    imag = pick(coupling[1][None, None, :]) * weight
    other = jnp.where(flag == 1, imag, -imag)
    op_hot = mode[:, :, None] % 3 == jnp.arange(3)[None, None, :]
    slot_hot = slot[:, :, None] == jnp.arange(slots)[None, None, :]
    both = op_hot[:, :, :, None] & slot_hot[:, :, None, :]

    def spread(values):
        return jnp.sum(jnp.where(both, values[:, :, None, None], 0.0), 1)

    creal, left, right = spread(real), spread(imag), spread(other)

    def parts(cimag):
        return jnp.stack([jnp.stack([creal, -cimag], -1), jnp.stack([cimag, creal], -1)], 1)

    table = jnp.stack([parts(left), parts(right)], 1)
    table = table.reshape(-1, slots * 2)
    table_high = table.astype(BF16)
    table_low = (table - table_high.astype(F32)).astype(BF16)
    pair = mode_hot[:, :, :, None] & slot_hot[:, :, None, :]
    corr = jnp.sum(jnp.where(pair, weight[:, :, None, None], 0.0), 1)
    return table_high, table_low, corr


def blown_up(table):
    tall, wide = table.shape
    down = (jnp.arange(tall * ROWS)[:, None] // ROWS == jnp.arange(tall)[None, :]).astype(BF16)
    along = (jnp.arange(wide)[:, None] == jnp.arange(wide * ROWS)[None, :] // ROWS).astype(BF16)
    big = jnp.dot(down, table, preferred_element_type=F32).astype(BF16)
    big = jnp.dot(big, along, preferred_element_type=F32)
    keep = jnp.arange(tall * ROWS)[:, None] % ROWS == jnp.arange(wide * ROWS)[None, :] % ROWS
    return jnp.where(keep, big, 0.0).astype(BF16)


def section_kernel(first, decay_ref, coef_ref, state_ref, near_ref, far_ref, ops_ref, before_ref, out_ref, corr_ref, mixed):
    count, _, width, _ = state_ref.shape
    slots = near_ref.shape[0] + far_ref.shape[0]
    corr_ref[...] = before_ref[...]

    @pl.loop(0, width // ROWS)
    def _(step):
        rows = pl.ds(pl.multiple_of(step * ROWS, ROWS), ROWS)
        chunk = jnp.concatenate([near_ref[:, :, rows, :], far_ref[:, :, rows, :]], 0)
        tall = chunk.reshape(slots * 2 * ROWS, width)
        sums = jnp.dot(coef_ref[0], tall, preferred_element_type=F32)
        sums += jnp.dot(coef_ref[1], tall, preferred_element_type=F32)
        sums = sums.astype(BF16)
        mixed[:, :, :, :, rows, :] = sums.reshape(count, 2, 2, 3, ROWS, width)
        for part in range(2):
            corr_ref[...] += lax.dot_general(
                state_ref[:, part, rows, :].reshape(count * ROWS, width),
                chunk[:, part].reshape(slots * ROWS, width),
                (((1,), (1,)), ((), ())),
                preferred_element_type=F32,
            )

    @pl.loop(0, count)
    def _(n):
        decay = decay_ref[n]
        for part in range(2):
            turned = -state_ref[n, 1] if part == 0 else state_ref[n, 0]
            rate = jnp.dot(ops_ref[0], turned, preferred_element_type=F32)
            for q in range(3):
                rate += jnp.dot(ops_ref[1 + q], mixed[n, 0, part, q], preferred_element_type=F32)
            back = jnp.dot(turned, ops_ref[0], preferred_element_type=F32)
            for q in range(3):
                back += jnp.dot(mixed[n, 1, part, q], ops_ref[1 + q], preferred_element_type=F32)
            own = state_ref[n, part].astype(F32)
            rate = rate - back - decay * own
            if first:
                out_ref[n, part] = (own + 0.125 * rate).astype(BF16)
            else:
                out_ref[n, part] = 0.25 * rate


def section(first, decay, coef, state, near, far, operators, before):
    count, _, width, _ = state.shape
    vmem = pl.BlockSpec(memory_space=pltpu.VMEM)
    return pl.pallas_call(
        functools.partial(section_kernel, first),
        out_shape=(
            jax.ShapeDtypeStruct(state.shape, BF16 if first else F32),
            jax.ShapeDtypeStruct(before.shape, F32),
        ),
        in_specs=[pl.BlockSpec(memory_space=pltpu.SMEM)] + [vmem] * 6,
        out_specs=(vmem, vmem),
        scratch_shapes=[pltpu.VMEM((count, 2, 2, 3, width, width), BF16)],
        compiler_params=pltpu.CompilerParams(vmem_limit_bytes=48 << 20),
        name="section_first" if first else "section_second",
    )(decay, coef, state, near, far, operators, before)


def greet(devices):
    barrier = pltpu.get_barrier_semaphore()
    for device in devices:
        pl.semaphore_signal(barrier, inc=1, device_id=device, device_id_type=MESH)
    pl.semaphore_wait(barrier, len(devices))


def remote(source, target, send, landed, device):
    return pltpu.make_async_remote_copy(
        src_ref=source,
        dst_ref=target,
        send_sem=send,
        recv_sem=landed,
        device_id=device,
        device_id_type=MESH,
    )


def exchange_kernel(tiers, whole, *refs):
    if whole:
        out_ref, state_ref, index_ref, near_ref, block_ref, other_ref, send, landed, own = refs
    else:
        out_ref, near_ref, send, landed, own = refs
    half = tiers // 2
    me, mat = lax.axis_index("tier"), lax.axis_index("mat")
    base = me // half * half
    local = me - base
    peers = [lax.rem(local + d, half) for d in range(1, half)]
    partner = (lax.rem(me + half, tiers), mat)
    greet([(base + peer, mat) for peer in peers] + ([partner] if whole else []))
    copies = []
    if whole:
        copies.append(remote(state_ref, block_ref, send.at[0], landed.at[0], partner))
        copies.append(remote(index_ref, other_ref, send.at[half], landed.at[half], partner))
    for d, peer in enumerate(peers, 1):
        copies.append(
            remote(out_ref.at[peer], near_ref.at[local], send.at[d], landed.at[d], (base + peer, mat))
        )
    keep = pltpu.make_async_copy(out_ref.at[local], near_ref.at[local], own)
    for copy in copies:
        copy.start()
    keep.start()
    for copy in copies:
        copy.wait()
    keep.wait()


def exchange(tiers, number, out, state=None, index=None):
    whole = state is not None
    args = (out, state, index) if whole else (out,)
    anywhere = pl.BlockSpec(memory_space=pl.ANY)
    half = tiers // 2
    return pl.pallas_call(
        functools.partial(exchange_kernel, tiers, whole),
        out_shape=tuple(jax.ShapeDtypeStruct(a.shape, a.dtype) for a in args),
        in_specs=[anywhere] * len(args),
        out_specs=(anywhere,) * len(args),
        scratch_shapes=[
            pltpu.SemaphoreType.DMA((half + 1,)),
            pltpu.SemaphoreType.DMA((half + 1,)),
            pltpu.SemaphoreType.DMA,
        ],
        compiler_params=pltpu.CompilerParams(collective_id=number, has_side_effects=True),
        name="exchange_whole" if whole else "exchange_half",
    )(*args)


def total_kernel(tiers, mats, value_ref, total_ref, by_tier, by_mat, middle, send, landed, send_mat, landed_mat):
    me, mat = lax.axis_index("tier"), lax.axis_index("mat")
    along = [(lax.rem(me + d, tiers), mat) for d in range(1, tiers)]
    across = [(me, lax.rem(mat + d, mats)) for d in range(1, mats)]
    greet(along + across)
    copies = [
        remote(value_ref, by_tier.at[me], send.at[d], landed.at[d], device)
        for d, device in enumerate(along)
    ]
    for copy in copies:
        copy.start()
    by_tier[me] = value_ref[...]
    for copy in copies:
        copy.wait()
    middle[...] = jnp.sum(by_tier[...], 0)
    by_mat[mat] = middle[...]
    copies = [
        remote(middle, by_mat.at[mat], send_mat.at[d], landed_mat.at[d], device)
        for d, device in enumerate(across)
    ]
    for copy in copies:
        copy.start()
    for copy in copies:
        copy.wait()
    total_ref[...] = jnp.sum(by_mat[...], 0)


def total(tiers, mats, number, value):
    vmem = pl.BlockSpec(memory_space=pltpu.VMEM)
    return pl.pallas_call(
        functools.partial(total_kernel, tiers, mats),
        out_shape=jax.ShapeDtypeStruct(value.shape, F32),
        in_specs=[vmem],
        out_specs=vmem,
        scratch_shapes=[
            pltpu.VMEM((tiers,) + value.shape, F32),
            pltpu.VMEM((mats,) + value.shape, F32),
            pltpu.VMEM(value.shape, F32),
            pltpu.SemaphoreType.DMA((tiers - 1,)),
            pltpu.SemaphoreType.DMA((tiers - 1,)),
            pltpu.SemaphoreType.DMA((mats - 1,)),
            pltpu.SemaphoreType.DMA((mats - 1,)),
        ],
        compiler_params=pltpu.CompilerParams(collective_id=number, has_side_effects=True),
        name="total",
    )(value)


def per_device(
    tiers,
    mats,
    costate,
    hamiltonian,
    couplers,
    damping,
    coupling,
    levels,
    neighbour_slot,
    neighbour_mode,
    neighbour_flag,
    send_index,
):
    count, _, width, _ = costate.shape
    slots = send_index.shape[1]
    half, cap = tiers // 2, slots // tiers
    me = lax.axis_index("tier")
    base = me // half * half

    def chosen(state, index):
        mine = lax.dynamic_slice(index[0], (base * cap,), (half * cap,))
        return state[mine].reshape((half, cap) + state.shape[1:])

    def flat(received):
        return received.reshape((half * cap,) + received.shape[2:])

    out = chosen(costate, send_index)
    near, block, other_index = exchange(tiers, 0, out, costate, send_index)
    (far,) = exchange(tiers, 1, chosen(block, other_index))
    operators = jnp.concatenate([symmetric(hamiltonian)[None], symmetric(couplers)], 0)
    nearest = (neighbour_slot + base * cap) % slots
    table_high, table_low, corr_weight = coefficients(
        coupling, levels, nearest, neighbour_mode, neighbour_flag, slots
    )
    coef = jnp.stack([blown_up(table_high), blown_up(table_low)])
    decay = jnp.sum(levels.astype(F32) * damping[None, :], 1)
    corr = jnp.zeros((count * ROWS, slots * ROWS), F32)
    middle, corr = section(True, decay, coef, costate, flat(near), flat(far), operators, corr)
    near, block, _ = exchange(tiers, 2, chosen(middle, send_index), middle, send_index)
    (far,) = exchange(tiers, 3, chosen(block, other_index))
    increment, corr = section(False, decay, coef, middle, flat(near), flat(far), operators, corr)
    row = jnp.arange(count * ROWS)[:, None]
    column = jnp.arange(slots * ROWS)[None, :]
    corr = jnp.where(row % ROWS == column % ROWS, corr, 0.0)
    pairs = jnp.sum(corr.reshape(count, ROWS, slots, ROWS), (1, 3)) / width
    grads = jnp.sum(pairs[:, None, :] * corr_weight, (0, 2))
    modes = grads.shape[0]
    padded = jnp.zeros((8, 128), F32).at[0, :modes].set(grads)
    return increment, total(tiers, mats, 4, padded)[0, :modes]


def solution(mesh):
    blocks = P(("tier", "mat"), None)
    return jax.shard_map(
        functools.partial(per_device, mesh.shape["tier"], mesh.shape["mat"]),
        mesh=mesh,
        in_specs=(P(("tier", "mat"), None, None, None), P(), P(), P(), P()) + (blocks,) * 5,
        out_specs=(P(("tier", "mat"), None, None, None), P()),
        check_vma=False,
    )
```

```python
import functools

import jax
import jax.numpy as jnp
from jax import lax
from jax.experimental import pallas as pl
from jax.experimental.pallas import tpu as pltpu
from jax.sharding import PartitionSpec as P

ROWS = 16
PIECES = 4
F32 = jnp.float32
BF16 = jnp.bfloat16
MESH = pl.DeviceIdType.MESH


def symmetric(weight):
    square = weight.astype(F32)
    return ((square + jnp.swapaxes(square, -1, -2)) * 0.5).astype(BF16)


def coefficients(coupling, levels, slot, mode, flag, slots):
    modes = levels.shape[1]
    mode_hot = mode[:, :, None] == jnp.arange(modes)[None, None, :]

    def pick(values):
        return jnp.sum(jnp.where(mode_hot, values, 0.0), -1)

    live = (flag >= 0).astype(F32)
    weight = jnp.sqrt(1.0 + pick(levels.astype(F32)[:, None, :])) * live
    real = pick(coupling[0][None, None, :]) * weight
    imag = pick(coupling[1][None, None, :]) * weight
    other = jnp.where(flag == 1, imag, -imag)
    op_hot = mode[:, :, None] % 3 == jnp.arange(3)[None, None, :]
    slot_hot = slot[:, :, None] == jnp.arange(slots)[None, None, :]
    both = op_hot[:, :, :, None] & slot_hot[:, :, None, :]

    def spread(values):
        return jnp.sum(jnp.where(both, values[:, :, None, None], 0.0), 1)

    creal, left, right = spread(real), spread(imag), spread(other)

    def parts(cimag):
        return jnp.stack([jnp.stack([creal, -cimag], -1), jnp.stack([cimag, creal], -1)], 1)

    table = jnp.stack([parts(left), parts(right)], 1)
    table = table.reshape(-1, slots * 2)
    high = lax.reduce_precision(table, 8, 7)
    table_high, table_low = high.astype(BF16), (table - high).astype(BF16)
    pair = mode_hot[:, :, :, None] & slot_hot[:, :, None, :]
    corr = jnp.sum(jnp.where(pair, weight[:, :, None, None], 0.0), 1)
    return table_high, table_low, corr


def blown_up(table):
    tall, wide = table.shape
    down = (jnp.arange(tall * ROWS)[:, None] // ROWS == jnp.arange(tall)[None, :]).astype(BF16)
    along = (jnp.arange(wide)[:, None] == jnp.arange(wide * ROWS)[None, :] // ROWS).astype(BF16)
    big = jnp.dot(down, table, preferred_element_type=F32).astype(BF16)
    big = jnp.dot(big, along, preferred_element_type=F32)
    keep = jnp.arange(tall * ROWS)[:, None] % ROWS == jnp.arange(wide * ROWS)[None, :] % ROWS
    return jnp.where(keep, big, 0.0).astype(BF16)


def greet(devices):
    barrier = pltpu.get_barrier_semaphore()
    for device in devices:
        pl.semaphore_signal(barrier, inc=1, device_id=device, device_id_type=MESH)
    pl.semaphore_wait(barrier, len(devices))


def remote(source, target, send, landed, device):
    return pltpu.make_async_remote_copy(
        src_ref=source,
        dst_ref=target,
        send_sem=send,
        recv_sem=landed,
        device_id=device,
        device_id_type=MESH,
    )


def section_kernel(
    tiers,
    first,
    decay_ref,
    index_ref,
    index_hbm,
    coef_ref,
    state_ref,
    ops_ref,
    before_ref,
    out_ref,
    corr_ref,
    other_hbm,
    mixed,
    acc,
    near_out,
    near,
    far_out,
    far,
    other,
    index_sems,
    block_send,
    block_land,
    near_send,
    near_land,
    far_send,
    far_land,
    *blocks,
):
    count, _, width, _ = state_ref.shape
    half, cap = near.shape[:2]
    slots = 2 * half * cap
    piece = width // PIECES
    me, mat = lax.axis_index("tier"), lax.axis_index("mat")
    base = me // half * half
    local = me - base
    peers = [lax.rem(local + d, half) for d in range(1, half)]
    partner = (lax.rem(me + half, tiers), mat)
    greet([(base + peer, mat) for peer in peers] + [partner])

    def span(k):
        return pl.ds(k * piece, piece)

    index_copy = remote(index_hbm, other_hbm, index_sems.at[0], index_sems.at[1], partner)
    index_copy.start()
    block_copies = [
        remote(
            state_ref.at[:, :, span(k), :],
            blocks[k],
            block_send.at[k],
            block_land.at[k],
            partner,
        )
        for k in range(PIECES)
    ]
    for copy in block_copies:
        copy.start()

    def to_peers(source, target, send, land, k):
        return [
            remote(
                source.at[peer, :, :, span(k), :],
                target.at[local, :, :, span(k), :],
                send.at[k, d],
                land.at[k, d],
                (base + peer, mat),
            )
            for d, peer in enumerate(peers)
        ]

    near_copies = [to_peers(near_out, near, near_send, near_land, k) for k in range(PIECES)]
    far_copies = [to_peers(far_out, far, far_send, far_land, k) for k in range(PIECES)]

    @pl.loop(0, half)
    def _(peer):
        for s in range(cap):
            near_out[peer, s] = state_ref[index_ref[0, (base + peer) * cap + s]]

    for copy in near_copies[0]:
        copy.start()
    for s in range(cap):
        near[local, s] = state_ref[index_ref[0, me * cap + s]]
    corr_ref[...] = before_ref[...]

    @pl.loop(0, count)
    def _(n):
        for part in range(2):
            turned = -state_ref[n, 1] if part == 0 else state_ref[n, 0]
            rate = jnp.dot(ops_ref[0], turned, preferred_element_type=F32)
            rate -= jnp.dot(turned, ops_ref[0], preferred_element_type=F32)
            acc[n, part] = rate - decay_ref[n] * state_ref[n, part].astype(F32)

    index_copy.wait()
    load_index = pltpu.make_async_copy(other_hbm, other, index_sems.at[2])
    load_index.start()
    load_index.wait()

    def forward(k):
        block_copies[k].wait_recv()

        @pl.loop(0, half)
        def _(peer):
            for s in range(cap):
                far_out[peer, s, :, span(k), :] = blocks[k][other[0, (base + peer) * cap + s]]

        for copy in far_copies[k]:
            copy.start()
        for s in range(cap):
            far[local, s, :, span(k), :] = blocks[k][other[0, me * cap + s]]

    def combine(k):
        for copy in near_copies[k] + far_copies[k]:
            copy.wait_recv()

        @pl.loop(0, piece // ROWS)
        def _(step):
            rows = pl.ds(pl.multiple_of(k * piece + step * ROWS, ROWS), ROWS)
            chunk = jnp.concatenate(
                [
                    near[:, :, :, rows, :].reshape(half * cap, 2, ROWS, width),
                    far[:, :, :, rows, :].reshape(half * cap, 2, ROWS, width),
                ],
                0,
            )
            tall = chunk.reshape(slots * 2 * ROWS, width)
            sums = jnp.dot(coef_ref[0], tall, preferred_element_type=F32)
            sums += jnp.dot(coef_ref[1], tall, preferred_element_type=F32)
            mixed[:, :, :, :, rows, :] = sums.astype(BF16).reshape(count, 2, 2, 3, ROWS, width)
            for part in range(2):
                corr_ref[...] += lax.dot_general(
                    state_ref[:, part, rows, :].reshape(count * ROWS, width),
                    chunk[:, part].reshape(slots * ROWS, width),
                    (((1,), (1,)), ((), ())),
                    preferred_element_type=F32,
                )

        for n in range(count):
            back = 0.0
            for q in range(3):
                right = mixed[n, 1, :, q, span(k), :].reshape(2 * piece, width)
                back += jnp.dot(right, ops_ref[1 + q], preferred_element_type=F32)
            acc[n, :, span(k), :] -= back.reshape(2, piece, width)

    for k in range(PIECES + 1):
        if k < PIECES:
            forward(k)
        if k + 1 < PIECES:
            for copy in near_copies[k + 1]:
                copy.start()
        if k > 0:
            combine(k - 1)

    @pl.loop(0, count)
    def _(n):
        for part in range(2):
            rate = acc[n, part]
            for q in range(3):
                rate += jnp.dot(ops_ref[1 + q], mixed[n, 0, part, q], preferred_element_type=F32)
            if first:
                out_ref[n, part] = (state_ref[n, part].astype(F32) + 0.125 * rate).astype(BF16)
            else:
                out_ref[n, part] = 0.25 * rate

    for k in range(PIECES):
        for copy in [block_copies[k]] + near_copies[k] + far_copies[k]:
            copy.wait_send()


def section(tiers, first, decay, index, coef, state, operators, before):
    count, _, width, _ = state.shape
    half, cap = tiers // 2, index.shape[1] // tiers
    vmem = pl.BlockSpec(memory_space=pltpu.VMEM)
    smem = pl.BlockSpec(memory_space=pltpu.SMEM)
    anywhere = pl.BlockSpec(memory_space=pl.ANY)
    slab = pltpu.VMEM((half, cap) + state.shape[1:], BF16)
    dma = pltpu.SemaphoreType.DMA
    return pl.pallas_call(
        functools.partial(section_kernel, tiers, first),
        out_shape=(
            jax.ShapeDtypeStruct(state.shape, BF16 if first else F32),
            jax.ShapeDtypeStruct(before.shape, F32),
            jax.ShapeDtypeStruct(index.shape, index.dtype),
        ),
        in_specs=[smem, smem, anywhere, vmem, vmem, vmem, vmem],
        out_specs=(vmem, vmem, anywhere),
        scratch_shapes=[
            pltpu.VMEM((count, 2, 2, 3, width, width), BF16),
            pltpu.VMEM(state.shape, F32),
            slab,
            slab,
            slab,
            slab,
            pltpu.SMEM(index.shape, index.dtype),
            dma((3,)),
            dma((PIECES,)),
            dma((PIECES,)),
        ]
        + [dma((PIECES, half - 1))] * 4
        + [pltpu.VMEM((count, 2, width // PIECES, width), BF16)] * PIECES,
        compiler_params=pltpu.CompilerParams(
            vmem_limit_bytes=56 << 20, collective_id=0 if first else 1, has_side_effects=True
        ),
        name="section_first" if first else "section_second",
    )(decay, index, index, coef, state, operators, before)


def total_kernel(tiers, mats, value_ref, total_ref, by_tier, by_mat, middle, send, landed, send_mat, landed_mat):
    me, mat = lax.axis_index("tier"), lax.axis_index("mat")
    along = [(lax.rem(me + d, tiers), mat) for d in range(1, tiers)]
    across = [(me, lax.rem(mat + d, mats)) for d in range(1, mats)]
    greet(along + across)
    copies = [
        remote(value_ref, by_tier.at[me], send.at[d], landed.at[d], device)
        for d, device in enumerate(along)
    ]
    for copy in copies:
        copy.start()
    by_tier[me] = value_ref[...]
    for copy in copies:
        copy.wait()
    middle[...] = jnp.sum(by_tier[...], 0)
    by_mat[mat] = middle[...]
    copies = [
        remote(middle, by_mat.at[mat], send_mat.at[d], landed_mat.at[d], device)
        for d, device in enumerate(across)
    ]
    for copy in copies:
        copy.start()
    for copy in copies:
        copy.wait()
    total_ref[...] = jnp.sum(by_mat[...], 0)


def total(tiers, mats, number, value):
    vmem = pl.BlockSpec(memory_space=pltpu.VMEM)
    return pl.pallas_call(
        functools.partial(total_kernel, tiers, mats),
        out_shape=jax.ShapeDtypeStruct(value.shape, F32),
        in_specs=[vmem],
        out_specs=vmem,
        scratch_shapes=[
            pltpu.VMEM((tiers,) + value.shape, F32),
            pltpu.VMEM((mats,) + value.shape, F32),
            pltpu.VMEM(value.shape, F32),
            pltpu.SemaphoreType.DMA((tiers - 1,)),
            pltpu.SemaphoreType.DMA((tiers - 1,)),
            pltpu.SemaphoreType.DMA((mats - 1,)),
            pltpu.SemaphoreType.DMA((mats - 1,)),
        ],
        compiler_params=pltpu.CompilerParams(collective_id=number, has_side_effects=True),
        name="total",
    )(value)


def per_device(
    tiers,
    mats,
    costate,
    hamiltonian,
    couplers,
    damping,
    coupling,
    levels,
    neighbour_slot,
    neighbour_mode,
    neighbour_flag,
    send_index,
):
    count, _, width, _ = costate.shape
    slots = send_index.shape[1]
    half, cap = tiers // 2, slots // tiers
    me = lax.axis_index("tier")
    base = me // half * half

    operators = jnp.concatenate([symmetric(hamiltonian)[None], symmetric(couplers)], 0)
    nearest = (neighbour_slot + base * cap) % slots
    table_high, table_low, corr_weight = coefficients(
        coupling, levels, nearest, neighbour_mode, neighbour_flag, slots
    )
    coef = jnp.stack([blown_up(table_high), blown_up(table_low)])
    decay = jnp.sum(levels.astype(F32) * damping[None, :], 1)
    corr = jnp.zeros((count * ROWS, slots * ROWS), F32)
    middle, corr, _ = section(tiers, True, decay, send_index, coef, costate, operators, corr)
    increment, corr, _ = section(tiers, False, decay, send_index, coef, middle, operators, corr)
    row = jnp.arange(count * ROWS)[:, None]
    column = jnp.arange(slots * ROWS)[None, :]
    corr = jnp.where(row % ROWS == column % ROWS, corr, 0.0)
    pairs = jnp.sum(corr.reshape(count, ROWS, slots, ROWS), (1, 3)) / width
    grads = jnp.sum(pairs[:, None, :] * corr_weight, (0, 2))
    modes = grads.shape[0]
    padded = jnp.zeros((8, 128), F32).at[0, :modes].set(grads)
    return increment, total(tiers, mats, 2, padded)[0, :modes]


def solution(mesh):
    blocks = P(("tier", "mat"), None)
    return jax.shard_map(
        functools.partial(per_device, mesh.shape["tier"], mesh.shape["mat"]),
        mesh=mesh,
        in_specs=(P(("tier", "mat"), None, None, None), P(), P(), P(), P()) + (blocks,) * 5,
        out_specs=(P(("tier", "mat"), None, None, None), P()),
        check_vma=False,
    )
```

```python
import functools

import jax
import jax.numpy as jnp
from jax import lax
from jax.experimental import pallas as pl
from jax.experimental.pallas import tpu as pltpu
from jax.sharding import PartitionSpec as P

ROWS = 16
PIECES = 8
F32 = jnp.float32
BF16 = jnp.bfloat16
MESH = pl.DeviceIdType.MESH


def symmetric(weight):
    square = weight.astype(F32)
    return ((square + jnp.swapaxes(square, -1, -2)) * 0.5).astype(BF16)


def coefficients(coupling, levels, slot, mode, flag, slots):
    modes = levels.shape[1]
    mode_hot = mode[:, :, None] == jnp.arange(modes)[None, None, :]

    def pick(values):
        return jnp.sum(jnp.where(mode_hot, values, 0.0), -1)

    live = (flag >= 0).astype(F32)
    weight = jnp.sqrt(1.0 + pick(levels.astype(F32)[:, None, :])) * live
    real = pick(coupling[0][None, None, :]) * weight
    imag = pick(coupling[1][None, None, :]) * weight
    other = jnp.where(flag == 1, imag, -imag)
    op_hot = mode[:, :, None] % 3 == jnp.arange(3)[None, None, :]
    slot_hot = slot[:, :, None] == jnp.arange(slots)[None, None, :]
    both = op_hot[:, :, :, None] & slot_hot[:, :, None, :]

    def spread(values):
        return jnp.sum(jnp.where(both, values[:, :, None, None], 0.0), 1)

    creal, left, right = spread(real), spread(imag), spread(other)

    def parts(cimag):
        return jnp.stack([jnp.stack([creal, -cimag], -1), jnp.stack([cimag, creal], -1)], 1)

    table = jnp.stack([parts(left), parts(right)], 1)
    table = table.reshape(-1, slots * 2)
    high = lax.reduce_precision(table, 8, 7)
    table_high, table_low = high.astype(BF16), (table - high).astype(BF16)
    pair = mode_hot[:, :, :, None] & slot_hot[:, :, None, :]
    corr = jnp.sum(jnp.where(pair, weight[:, :, None, None], 0.0), 1)
    return table_high, table_low, corr


def blow_up(table_ref, coef_ref):
    _, tall, wide = table_ref.shape
    bits = ROWS.bit_length() - 1

    def iota(shape, axis):
        return lax.broadcasted_iota(jnp.int32, shape, axis)

    def hot(keep):
        return jnp.where(keep, 1.0, 0.0).astype(BF16)

    shape = (tall * ROWS, tall)
    down = hot(iota(shape, 0) >> bits == iota(shape, 1))
    shape = (wide, wide * ROWS)
    along = hot(iota(shape, 0) == iota(shape, 1) >> bits)
    shape = (tall * ROWS, wide * ROWS)
    keep = iota(shape, 0) & (ROWS - 1) == iota(shape, 1) & (ROWS - 1)
    for half in range(2):
        big = jnp.dot(down, table_ref[half], preferred_element_type=F32).astype(BF16)
        big = jnp.dot(big, along, preferred_element_type=F32)
        coef_ref[half] = jnp.where(keep, big, 0.0).astype(BF16)


def greet(devices):
    barrier = pltpu.get_barrier_semaphore()
    for device in devices:
        pl.semaphore_signal(barrier, inc=1, device_id=device, device_id_type=MESH)
    pl.semaphore_wait(barrier, len(devices))


def remote(source, target, send, landed, device):
    return pltpu.make_async_remote_copy(
        src_ref=source,
        dst_ref=target,
        send_sem=send,
        recv_sem=landed,
        device_id=device,
        device_id_type=MESH,
    )


def section_kernel(
    tiers,
    first,
    decay_ref,
    index_ref,
    index_hbm,
    table_ref,
    state_ref,
    ops_ref,
    before_ref,
    out_ref,
    corr_ref,
    other_hbm,
    coef_ref,
    mixed,
    acc,
    near_out,
    near,
    far_out,
    far,
    other,
    index_sems,
    block_send,
    block_land,
    near_send,
    near_land,
    far_send,
    far_land,
    *blocks,
):
    count, _, width, _ = state_ref.shape
    half, cap = near.shape[:2]
    slots = 2 * half * cap
    piece = width // PIECES
    me, mat = lax.axis_index("tier"), lax.axis_index("mat")
    base = me // half * half
    local = me - base
    peers = [lax.rem(local + d, half) for d in range(1, half)]
    partner = (lax.rem(me + half, tiers), mat)
    greet([(base + peer, mat) for peer in peers] + [partner])

    def span(k):
        return pl.ds(k * piece, piece)

    index_copy = remote(index_hbm, other_hbm, index_sems.at[0], index_sems.at[1], partner)
    index_copy.start()
    block_copies = [
        remote(
            state_ref.at[:, :, span(k), :],
            blocks[k],
            block_send.at[k],
            block_land.at[k],
            partner,
        )
        for k in range(PIECES)
    ]
    for copy in block_copies:
        copy.start()

    def to_peers(source, target, send, land, k):
        return [
            remote(
                source.at[peer, :, :, span(k), :],
                target.at[local, :, :, span(k), :],
                send.at[k, d],
                land.at[k, d],
                (base + peer, mat),
            )
            for d, peer in enumerate(peers)
        ]

    near_copies = [to_peers(near_out, near, near_send, near_land, k) for k in range(PIECES)]
    far_copies = [to_peers(far_out, far, far_send, far_land, k) for k in range(PIECES)]

    @pl.loop(0, half)
    def _(peer):
        for s in range(cap):
            near_out[peer, s] = state_ref[index_ref[0, (base + peer) * cap + s]]

    for copy in near_copies[0]:
        copy.start()
    for s in range(cap):
        near[local, s] = state_ref[index_ref[0, me * cap + s]]
    corr_ref[...] = jnp.zeros_like(corr_ref) if first else before_ref[...]
    blow_up(table_ref, coef_ref)

    @pl.loop(0, count)
    def _(n):
        for part in range(2):
            turned = -state_ref[n, 1] if part == 0 else state_ref[n, 0]
            rate = jnp.dot(ops_ref[0], turned, preferred_element_type=F32)
            rate -= jnp.dot(turned, ops_ref[0], preferred_element_type=F32)
            acc[n, part] = rate - decay_ref[n] * state_ref[n, part].astype(F32)

    index_copy.wait()
    load_index = pltpu.make_async_copy(other_hbm, other, index_sems.at[2])
    load_index.start()
    load_index.wait()

    def forward(k):
        block_copies[k].wait_recv()

        @pl.loop(0, half)
        def _(peer):
            for s in range(cap):
                far_out[peer, s, :, span(k), :] = blocks[k][other[0, (base + peer) * cap + s]]

        for copy in far_copies[k]:
            copy.start()
        for s in range(cap):
            far[local, s, :, span(k), :] = blocks[k][other[0, me * cap + s]]

    def combine(k):
        for copy in near_copies[k] + far_copies[k]:
            copy.wait_recv()

        @pl.loop(0, piece // ROWS)
        def _(step):
            rows = pl.ds(pl.multiple_of(k * piece + step * ROWS, ROWS), ROWS)
            chunk = jnp.concatenate(
                [
                    near[:, :, :, rows, :].reshape(half * cap, 2, ROWS, width),
                    far[:, :, :, rows, :].reshape(half * cap, 2, ROWS, width),
                ],
                0,
            )
            tall = chunk.reshape(slots * 2 * ROWS, width)
            sums = jnp.dot(coef_ref[0], tall, preferred_element_type=F32)
            sums += jnp.dot(coef_ref[1], tall, preferred_element_type=F32)
            mixed[:, :, :, :, rows, :] = sums.astype(BF16).reshape(count, 2, 2, 3, ROWS, width)
            for part in range(2):
                corr_ref[...] += lax.dot_general(
                    state_ref[:, part, rows, :].reshape(count * ROWS, width),
                    chunk[:, part].reshape(slots * ROWS, width),
                    (((1,), (1,)), ((), ())),
                    preferred_element_type=F32,
                )

        for n in range(count):
            back = 0.0
            for q in range(3):
                right = mixed[n, 1, :, q, span(k), :].reshape(2 * piece, width)
                back += jnp.dot(right, ops_ref[1 + q], preferred_element_type=F32)
            acc[n, :, span(k), :] -= back.reshape(2, piece, width)

    for k in range(PIECES + 1):
        if k < PIECES:
            forward(k)
        if k + 1 < PIECES:
            for copy in near_copies[k + 1]:
                copy.start()
        if k > 0:
            combine(k - 1)

    @pl.loop(0, count)
    def _(n):
        for part in range(2):
            rate = acc[n, part]
            for q in range(3):
                rate += jnp.dot(ops_ref[1 + q], mixed[n, 0, part, q], preferred_element_type=F32)
            if first:
                out_ref[n, part] = (state_ref[n, part].astype(F32) + 0.125 * rate).astype(BF16)
            else:
                out_ref[n, part] = 0.25 * rate

    for k in range(PIECES):
        for copy in [block_copies[k]] + near_copies[k] + far_copies[k]:
            copy.wait_send()


def section(tiers, first, decay, index, coef, state, operators, before):
    count, _, width, _ = state.shape
    half, cap = tiers // 2, index.shape[1] // tiers
    vmem = pl.BlockSpec(memory_space=pltpu.VMEM)
    smem = pl.BlockSpec(memory_space=pltpu.SMEM)
    anywhere = pl.BlockSpec(memory_space=pl.ANY)
    slab = pltpu.VMEM((half, cap) + state.shape[1:], BF16)
    dma = pltpu.SemaphoreType.DMA
    return pl.pallas_call(
        functools.partial(section_kernel, tiers, first),
        out_shape=(
            jax.ShapeDtypeStruct(state.shape, BF16 if first else F32),
            jax.ShapeDtypeStruct(before.shape, F32),
            jax.ShapeDtypeStruct(index.shape, index.dtype),
        ),
        in_specs=[smem, smem, anywhere, vmem, vmem, vmem, vmem],
        out_specs=(vmem, vmem, anywhere),
        scratch_shapes=[
            pltpu.VMEM((2, coef.shape[1] * ROWS, coef.shape[2] * ROWS), BF16),
            pltpu.VMEM((count, 2, 2, 3, width, width), BF16),
            pltpu.VMEM(state.shape, F32),
            slab,
            slab,
            slab,
            slab,
            pltpu.SMEM(index.shape, index.dtype),
            dma((3,)),
            dma((PIECES,)),
            dma((PIECES,)),
        ]
        + [dma((PIECES, half - 1))] * 4
        + [pltpu.VMEM((count, 2, width // PIECES, width), BF16)] * PIECES,
        compiler_params=pltpu.CompilerParams(
            vmem_limit_bytes=56 << 20, collective_id=0 if first else 1, has_side_effects=True
        ),
        name="section_first" if first else "section_second",
    )(decay, index, index, coef, state, operators, before)


def total_kernel(tiers, mats, value_ref, total_ref, by_tier, by_mat, middle, send, landed, send_mat, landed_mat):
    me, mat = lax.axis_index("tier"), lax.axis_index("mat")
    along = [(lax.rem(me + d, tiers), mat) for d in range(1, tiers)]
    across = [(me, lax.rem(mat + d, mats)) for d in range(1, mats)]
    greet(along + across)
    copies = [
        remote(value_ref, by_tier.at[me], send.at[d], landed.at[d], device)
        for d, device in enumerate(along)
    ]
    for copy in copies:
        copy.start()
    by_tier[me] = value_ref[...]
    for copy in copies:
        copy.wait()
    middle[...] = jnp.sum(by_tier[...], 0)
    by_mat[mat] = middle[...]
    copies = [
        remote(middle, by_mat.at[mat], send_mat.at[d], landed_mat.at[d], device)
        for d, device in enumerate(across)
    ]
    for copy in copies:
        copy.start()
    for copy in copies:
        copy.wait()
    total_ref[...] = jnp.sum(by_mat[...], 0)


def total(tiers, mats, number, value):
    vmem = pl.BlockSpec(memory_space=pltpu.VMEM)
    return pl.pallas_call(
        functools.partial(total_kernel, tiers, mats),
        out_shape=jax.ShapeDtypeStruct(value.shape, F32),
        in_specs=[vmem],
        out_specs=vmem,
        scratch_shapes=[
            pltpu.VMEM((tiers,) + value.shape, F32),
            pltpu.VMEM((mats,) + value.shape, F32),
            pltpu.VMEM(value.shape, F32),
            pltpu.SemaphoreType.DMA((tiers - 1,)),
            pltpu.SemaphoreType.DMA((tiers - 1,)),
            pltpu.SemaphoreType.DMA((mats - 1,)),
            pltpu.SemaphoreType.DMA((mats - 1,)),
        ],
        compiler_params=pltpu.CompilerParams(collective_id=number, has_side_effects=True),
        name="total",
    )(value)


def per_device(
    tiers,
    mats,
    costate,
    hamiltonian,
    couplers,
    damping,
    coupling,
    levels,
    neighbour_slot,
    neighbour_mode,
    neighbour_flag,
    send_index,
):
    count, _, width, _ = costate.shape
    slots = send_index.shape[1]
    half, cap = tiers // 2, slots // tiers
    me = lax.axis_index("tier")
    base = me // half * half

    operators = jnp.concatenate([symmetric(hamiltonian)[None], symmetric(couplers)], 0)
    nearest = (neighbour_slot + base * cap) % slots
    table_high, table_low, corr_weight = coefficients(
        coupling, levels, nearest, neighbour_mode, neighbour_flag, slots
    )
    coef = jnp.stack([table_high, table_low])
    decay = jnp.sum(levels.astype(F32) * damping[None, :], 1)
    corr = jnp.zeros((count * ROWS, slots * ROWS), F32)
    middle, corr, _ = section(tiers, True, decay, send_index, coef, costate, operators, corr)
    increment, corr, _ = section(tiers, False, decay, send_index, coef, middle, operators, corr)
    row = jnp.arange(count * ROWS)[:, None]
    column = jnp.arange(slots * ROWS)[None, :]
    corr = jnp.where(row % ROWS == column % ROWS, corr, 0.0)
    pairs = jnp.sum(corr.reshape(count, ROWS, slots, ROWS), (1, 3)) / width
    grads = jnp.sum(pairs[:, None, :] * corr_weight, (0, 2))
    modes = grads.shape[0]
    padded = jnp.zeros((8, 128), F32).at[0, :modes].set(grads)
    return increment, total(tiers, mats, 2, padded)[0, :modes]


def solution(mesh):
    blocks = P(("tier", "mat"), None)
    return jax.shard_map(
        functools.partial(per_device, mesh.shape["tier"], mesh.shape["mat"]),
        mesh=mesh,
        in_specs=(P(("tier", "mat"), None, None, None), P(), P(), P(), P()) + (blocks,) * 5,
        out_specs=(P(("tier", "mat"), None, None, None), P()),
        check_vma=False,
    )
```

```python
import functools

import jax
import jax.numpy as jnp
from jax import lax
from jax.experimental import pallas as pl
from jax.experimental.pallas import tpu as pltpu
from jax.sharding import PartitionSpec as P

ROWS = 16
PIECES = 2
F32 = jnp.float32
BF16 = jnp.bfloat16
MESH = pl.DeviceIdType.MESH


def symmetric(weight):
    square = weight.astype(F32)
    return ((square + jnp.swapaxes(square, -1, -2)) * 0.5).astype(BF16)


def coefficients(coupling, levels, slot, mode, flag, slots):
    modes = levels.shape[1]
    mode_hot = mode[:, :, None] == jnp.arange(modes)[None, None, :]

    def pick(values):
        return jnp.sum(jnp.where(mode_hot, values, 0.0), -1)

    live = (flag >= 0).astype(F32)
    weight = jnp.sqrt(1.0 + pick(levels.astype(F32)[:, None, :])) * live
    real = pick(coupling[0][None, None, :]) * weight
    imag = pick(coupling[1][None, None, :]) * weight
    other = jnp.where(flag == 1, imag, -imag)
    op_hot = mode[:, :, None] % 3 == jnp.arange(3)[None, None, :]
    slot_hot = slot[:, :, None] == jnp.arange(slots)[None, None, :]
    both = op_hot[:, :, :, None] & slot_hot[:, :, None, :]

    def spread(values):
        return jnp.sum(jnp.where(both, values[:, :, None, None], 0.0), 1)

    creal, left, right = spread(real), spread(imag), spread(other)

    def parts(cimag):
        return jnp.stack([jnp.stack([creal, -cimag], -1), jnp.stack([cimag, creal], -1)], 1)

    table = jnp.stack([parts(left), parts(right)], 1)
    table = table.reshape(-1, slots * 2)
    high = lax.reduce_precision(table, 8, 7)
    table_high, table_low = high.astype(BF16), (table - high).astype(BF16)
    pair = mode_hot[:, :, :, None] & slot_hot[:, :, None, :]
    corr = jnp.sum(jnp.where(pair, weight[:, :, None, None], 0.0), 1)
    return table_high, table_low, corr


def blown_up(table):
    tall, wide = table.shape
    down = (jnp.arange(tall * ROWS)[:, None] // ROWS == jnp.arange(tall)[None, :]).astype(BF16)
    along = (jnp.arange(wide)[:, None] == jnp.arange(wide * ROWS)[None, :] // ROWS).astype(BF16)
    big = jnp.dot(down, table, preferred_element_type=F32).astype(BF16)
    big = jnp.dot(big, along, preferred_element_type=F32)
    keep = jnp.arange(tall * ROWS)[:, None] % ROWS == jnp.arange(wide * ROWS)[None, :] % ROWS
    return jnp.where(keep, big, 0.0).astype(BF16)


def greet(devices):
    barrier = pltpu.get_barrier_semaphore()
    for device in devices:
        pl.semaphore_signal(barrier, inc=1, device_id=device, device_id_type=MESH)
    pl.semaphore_wait(barrier, len(devices))


def remote(source, target, send, landed, device):
    return pltpu.make_async_remote_copy(
        src_ref=source,
        dst_ref=target,
        send_sem=send,
        recv_sem=landed,
        device_id=device,
        device_id_type=MESH,
    )


def section_kernel(
    tiers,
    first,
    decay_ref,
    index_ref,
    index_hbm,
    coef_ref,
    state_ref,
    ops_ref,
    before_ref,
    out_ref,
    corr_ref,
    other_hbm,
    mixed,
    acc,
    near_out,
    near,
    far_out,
    far,
    other,
    index_sems,
    block_send,
    block_land,
    near_send,
    near_land,
    far_send,
    far_land,
    *blocks,
):
    count, _, width, _ = state_ref.shape
    half, cap = near.shape[:2]
    slots = 2 * half * cap
    piece = width // PIECES
    me, mat = lax.axis_index("tier"), lax.axis_index("mat")
    base = me // half * half
    local = me - base
    peers = [lax.rem(local + d, half) for d in range(1, half)]
    partner = (lax.rem(me + half, tiers), mat)
    greet([(base + peer, mat) for peer in peers] + [partner])

    def span(k):
        return pl.ds(k * piece, piece)

    index_copy = remote(index_hbm, other_hbm, index_sems.at[0], index_sems.at[1], partner)
    index_copy.start()
    block_copies = [
        remote(
            state_ref.at[:, :, span(k), :],
            blocks[k],
            block_send.at[k],
            block_land.at[k],
            partner,
        )
        for k in range(PIECES)
    ]
    for copy in block_copies:
        copy.start()

    def to_peers(source, target, send, land, k):
        return [
            remote(
                source.at[peer, :, :, span(k), :],
                target.at[local, :, :, span(k), :],
                send.at[k, d],
                land.at[k, d],
                (base + peer, mat),
            )
            for d, peer in enumerate(peers)
        ]

    near_copies = [to_peers(near_out, near, near_send, near_land, k) for k in range(PIECES)]
    far_copies = [to_peers(far_out, far, far_send, far_land, k) for k in range(PIECES)]

    @pl.loop(0, half)
    def _(peer):
        for s in range(cap):
            near_out[peer, s] = state_ref[index_ref[0, (base + peer) * cap + s]]

    for copy in near_copies[0]:
        copy.start()
    for s in range(cap):
        near[local, s] = state_ref[index_ref[0, me * cap + s]]
    corr_ref[...] = before_ref[...]

    @pl.loop(0, count)
    def _(n):
        for part in range(2):
            turned = -state_ref[n, 1] if part == 0 else state_ref[n, 0]
            rate = jnp.dot(ops_ref[0], turned, preferred_element_type=F32)
            rate -= jnp.dot(turned, ops_ref[0], preferred_element_type=F32)
            acc[n, part] = rate - decay_ref[n] * state_ref[n, part].astype(F32)

    index_copy.wait()
    load_index = pltpu.make_async_copy(other_hbm, other, index_sems.at[2])
    load_index.start()
    load_index.wait()

    def forward(k):
        block_copies[k].wait_recv()

        @pl.loop(0, half)
        def _(peer):
            for s in range(cap):
                far_out[peer, s, :, span(k), :] = blocks[k][other[0, (base + peer) * cap + s]]

        for copy in far_copies[k]:
            copy.start()
        for s in range(cap):
            far[local, s, :, span(k), :] = blocks[k][other[0, me * cap + s]]

    def combine(k):
        for copy in near_copies[k] + far_copies[k]:
            copy.wait_recv()

        @pl.loop(0, piece // ROWS)
        def _(step):
            rows = pl.ds(pl.multiple_of(k * piece + step * ROWS, ROWS), ROWS)
            chunk = jnp.concatenate(
                [
                    near[:, :, :, rows, :].reshape(half * cap, 2, ROWS, width),
                    far[:, :, :, rows, :].reshape(half * cap, 2, ROWS, width),
                ],
                0,
            )
            tall = chunk.reshape(slots * 2 * ROWS, width)
            sums = jnp.dot(coef_ref[0], tall, preferred_element_type=F32)
            sums += jnp.dot(coef_ref[1], tall, preferred_element_type=F32)
            mixed[:, :, :, :, rows, :] = sums.astype(BF16).reshape(count, 2, 2, 3, ROWS, width)
            for part in range(2):
                corr_ref[...] += lax.dot_general(
                    state_ref[:, part, rows, :].reshape(count * ROWS, width),
                    chunk[:, part].reshape(slots * ROWS, width),
                    (((1,), (1,)), ((), ())),
                    preferred_element_type=F32,
                )

        for n in range(count):
            back = 0.0
            for q in range(3):
                right = mixed[n, 1, :, q, span(k), :].reshape(2 * piece, width)
                back += jnp.dot(right, ops_ref[1 + q], preferred_element_type=F32)
            acc[n, :, span(k), :] -= back.reshape(2, piece, width)

    for k in range(PIECES + 1):
        if k < PIECES:
            forward(k)
        if k + 1 < PIECES:
            for copy in near_copies[k + 1]:
                copy.start()
        if k > 0:
            combine(k - 1)

    @pl.loop(0, count)
    def _(n):
        for part in range(2):
            rate = acc[n, part]
            for q in range(3):
                rate += jnp.dot(ops_ref[1 + q], mixed[n, 0, part, q], preferred_element_type=F32)
            if first:
                out_ref[n, part] = (state_ref[n, part].astype(F32) + 0.125 * rate).astype(BF16)
            else:
                out_ref[n, part] = 0.25 * rate

    for k in range(PIECES):
        for copy in [block_copies[k]] + near_copies[k] + far_copies[k]:
            copy.wait_send()


def section(tiers, first, decay, index, coef, state, operators, before):
    count, _, width, _ = state.shape
    half, cap = tiers // 2, index.shape[1] // tiers
    vmem = pl.BlockSpec(memory_space=pltpu.VMEM)
    smem = pl.BlockSpec(memory_space=pltpu.SMEM)
    anywhere = pl.BlockSpec(memory_space=pl.ANY)
    slab = pltpu.VMEM((half, cap) + state.shape[1:], BF16)
    dma = pltpu.SemaphoreType.DMA
    return pl.pallas_call(
        functools.partial(section_kernel, tiers, first),
        out_shape=(
            jax.ShapeDtypeStruct(state.shape, BF16 if first else F32),
            jax.ShapeDtypeStruct(before.shape, F32),
            jax.ShapeDtypeStruct(index.shape, index.dtype),
        ),
        in_specs=[smem, smem, anywhere, vmem, vmem, vmem, vmem],
        out_specs=(vmem, vmem, anywhere),
        scratch_shapes=[
            pltpu.VMEM((count, 2, 2, 3, width, width), BF16),
            pltpu.VMEM(state.shape, F32),
            slab,
            slab,
            slab,
            slab,
            pltpu.SMEM(index.shape, index.dtype),
            dma((3,)),
            dma((PIECES,)),
            dma((PIECES,)),
        ]
        + [dma((PIECES, half - 1))] * 4
        + [pltpu.VMEM((count, 2, width // PIECES, width), BF16)] * PIECES,
        compiler_params=pltpu.CompilerParams(
            vmem_limit_bytes=56 << 20, collective_id=0 if first else 1, has_side_effects=True
        ),
        name="section_first" if first else "section_second",
    )(decay, index, index, coef, state, operators, before)


def total_kernel(tiers, mats, value_ref, total_ref, by_tier, by_mat, middle, send, landed, send_mat, landed_mat):
    me, mat = lax.axis_index("tier"), lax.axis_index("mat")
    along = [(lax.rem(me + d, tiers), mat) for d in range(1, tiers)]
    across = [(me, lax.rem(mat + d, mats)) for d in range(1, mats)]
    greet(along + across)
    copies = [
        remote(value_ref, by_tier.at[me], send.at[d], landed.at[d], device)
        for d, device in enumerate(along)
    ]
    for copy in copies:
        copy.start()
    by_tier[me] = value_ref[...]
    for copy in copies:
        copy.wait()
    middle[...] = jnp.sum(by_tier[...], 0)
    by_mat[mat] = middle[...]
    copies = [
        remote(middle, by_mat.at[mat], send_mat.at[d], landed_mat.at[d], device)
        for d, device in enumerate(across)
    ]
    for copy in copies:
        copy.start()
    for copy in copies:
        copy.wait()
    total_ref[...] = jnp.sum(by_mat[...], 0)


def total(tiers, mats, number, value):
    vmem = pl.BlockSpec(memory_space=pltpu.VMEM)
    return pl.pallas_call(
        functools.partial(total_kernel, tiers, mats),
        out_shape=jax.ShapeDtypeStruct(value.shape, F32),
        in_specs=[vmem],
        out_specs=vmem,
        scratch_shapes=[
            pltpu.VMEM((tiers,) + value.shape, F32),
            pltpu.VMEM((mats,) + value.shape, F32),
            pltpu.VMEM(value.shape, F32),
            pltpu.SemaphoreType.DMA((tiers - 1,)),
            pltpu.SemaphoreType.DMA((tiers - 1,)),
            pltpu.SemaphoreType.DMA((mats - 1,)),
            pltpu.SemaphoreType.DMA((mats - 1,)),
        ],
        compiler_params=pltpu.CompilerParams(collective_id=number, has_side_effects=True),
        name="total",
    )(value)


def per_device(
    tiers,
    mats,
    costate,
    hamiltonian,
    couplers,
    damping,
    coupling,
    levels,
    neighbour_slot,
    neighbour_mode,
    neighbour_flag,
    send_index,
):
    count, _, width, _ = costate.shape
    slots = send_index.shape[1]
    half, cap = tiers // 2, slots // tiers
    me = lax.axis_index("tier")
    base = me // half * half

    operators = jnp.concatenate([symmetric(hamiltonian)[None], symmetric(couplers)], 0)
    nearest = (neighbour_slot + base * cap) % slots
    table_high, table_low, corr_weight = coefficients(
        coupling, levels, nearest, neighbour_mode, neighbour_flag, slots
    )
    coef = jnp.stack([blown_up(table_high), blown_up(table_low)])
    decay = jnp.sum(levels.astype(F32) * damping[None, :], 1)
    corr = jnp.zeros((count * ROWS, slots * ROWS), F32)
    middle, corr, _ = section(tiers, True, decay, send_index, coef, costate, operators, corr)
    increment, corr, _ = section(tiers, False, decay, send_index, coef, middle, operators, corr)
    row = jnp.arange(count * ROWS)[:, None]
    column = jnp.arange(slots * ROWS)[None, :]
    corr = jnp.where(row % ROWS == column % ROWS, corr, 0.0)
    pairs = jnp.sum(corr.reshape(count, ROWS, slots, ROWS), (1, 3)) / width
    grads = jnp.sum(pairs[:, None, :] * corr_weight, (0, 2))
    modes = grads.shape[0]
    padded = jnp.zeros((8, 128), F32).at[0, :modes].set(grads)
    return increment, total(tiers, mats, 2, padded)[0, :modes]


def solution(mesh):
    blocks = P(("tier", "mat"), None)
    return jax.shard_map(
        functools.partial(per_device, mesh.shape["tier"], mesh.shape["mat"]),
        mesh=mesh,
        in_specs=(P(("tier", "mat"), None, None, None), P(), P(), P(), P()) + (blocks,) * 5,
        out_specs=(P(("tier", "mat"), None, None, None), P()),
        check_vma=False,
    )
```
